32 devices in a mesh: groups: 2 (over x), seq: 16 (over z, y, core).
Axes of the slice: x: 2, y: 2, z: 4, core: 2. Of those that a mesh axis runs over, the one named last changes fastest.
Arguments:
- queries: bfloat16 [4, 2048, 4096], P('groups', 'seq'), parts along dimension 0, may hold values from -120 to 120
- key_states: bfloat16 [4, 2048, 4096], P('groups', 'seq'), parts along dimension 0, may hold values from -4 to 4
- value_states: bfloat16 [4, 2048, 4096], P('groups', 'seq'), parts along dimension 0, may hold values from -6 to 6
- random_blocks: int32 [4, 32, 3], P('groups'), parts along dimension 0, may hold values from 0 to 31
- global_blocks: int32 [4, 2], P('groups'), parts along dimension 0, may hold values from 0 to 31, as said below
Outputs:
- attended: bfloat16 [4, 2048, 4096], P('groups', 'seq'), parts along dimension 0
The draws below stay inside these ranges and needn't reach their ends.
There are 2 independent parts, one for each index of `groups`. The reference program is written for one: setup_inputs(seed, part) draws one part's arguments, and reference() takes and returns one part's arrays. A program takes and returns all parts, laid end to end along the dimension named above; each array names one. Nothing has to cross between parts.
Inputs may be any that keep to these rules, and one draw needn't show every extreme that they name: `global_blocks`: the 2 global blocks of a document are different, the first below 16 and the second not.
All inputs are finite; a program needn't handle non-finite values.
Results may differ from the reference program's by a relative error of at most 0.008.
Values may be sent and summed in bfloat16 or wider, within the bound.
A program may use at most 128 MiB of HBM per device.

```python
import math
import jax
import jax.numpy as jnp
from jax import lax

HEADS = 32
HEAD_DIM = 128
BLOCK = 64
NGLOB = 2
NRAND = 3
DOCS = 2
NBLK = 32
LEN = 2048
ATT = 4096


def drawn_parts(key):
    base = jnp.clip(jax.random.normal(jax.random.fold_in(key, 7), (DOCS, LEN, ATT), jnp.float32), -4.0, 4.0)
    return base


def draw_key_states(key, part):
    base = drawn_parts(key)
    return base.astype(jnp.bfloat16)


def draw_queries(key, part):
    fresh = jnp.clip(jax.random.normal(jax.random.fold_in(key, 5), (DOCS, LEN, ATT), jnp.float32), -4.0, 4.0)
    return fresh.astype(jnp.bfloat16)


def draw_global_blocks(key, part):
    lower = jax.random.randint(jax.random.fold_in(key, 3), (DOCS, 1), 0, NBLK // 2)
    upper = jax.random.randint(jax.random.fold_in(key, 4), (DOCS, 1), NBLK // 2, NBLK)
    documents = jnp.arange(DOCS, dtype=jnp.int32)[:, None]
    high_pick = jax.random.randint(jax.random.fold_in(key, 6), (), 0, DOCS)
    low_pick = jax.random.randint(jax.random.fold_in(key, 8), (), 0, DOCS)
    upper = jnp.where(documents == high_pick, NBLK - 1, upper)
    lower = jnp.where(documents == low_pick, 0, lower)
    return jnp.concatenate([lower, upper], axis=1).astype(jnp.int32)


def touch_ends(values, rng, low, top_value):
    longest = values.shape.index(max(values.shape))
    spots = []
    for shift in (0, 1):
        where = [jax.random.randint(jax.random.fold_in(rng, axis), (), 0, length) for axis, length in enumerate(values.shape)]
        where[longest] = (where[longest] + shift) % values.shape[longest]
        spots.append(tuple(where))
    return values.at[spots[0]].set(low).at[spots[1]].set(top_value)


def block_scale(rng, shape, shards, low, high):
    factor_of, own = 1.0, jax.random.fold_in(rng, 6)
    for dim, parts in shards:
        draws = jnp.exp(jax.random.uniform(jax.random.fold_in(own, dim), (parts,), jnp.float32, low / len(shards), high / len(shards)))
        factor_of = factor_of * jnp.repeat(draws, shape[dim] // parts).reshape([-1 if axis == dim else 1 for axis in range(len(shape))])
    return factor_of


def normal_values(stream_key, shape, deviation, bound, cuts=(), kind=jnp.bfloat16):
    gain = block_scale(stream_key, shape, cuts, -0.22, 0.18) if cuts else 1.0
    drawn = jax.random.normal(stream_key, shape, jnp.float32) * deviation * gain
    return jnp.minimum(jnp.maximum(drawn, -bound), bound).astype(kind)


def setup_inputs(seed: int = 0, part: int = 0) -> dict:
    seeds = jax.random.split(jax.random.key(seed), 6)
    part_keys = jax.random.split(jax.random.fold_in(seeds[5], part), 6)
    return {
        "queries": draw_queries(jax.random.fold_in(jax.random.fold_in(seeds[5], part), 71), part),
        "key_states": draw_key_states(jax.random.fold_in(jax.random.fold_in(seeds[5], part), 71), part),
        "value_states": normal_values(part_keys[2], (DOCS, LEN, ATT), 1.0, 6.0, ((1, 16),)),
        "random_blocks": touch_ends(jax.random.randint(part_keys[3], (DOCS, NBLK, NRAND), 0, NBLK), jax.random.fold_in(part_keys[3], 1), 0, NBLK - 1).astype(jnp.int32),
        "global_blocks": draw_global_blocks(jax.random.fold_in(jax.random.fold_in(seeds[5], part), 71), part),
    }


def soft_weights(scores):
    row_max = jnp.max(scores, axis=-1, keepdims=True)
    exponent = jnp.exp(scores - row_max)
    return (exponent / jnp.sum(exponent, axis=-1, keepdims=True)).astype(jnp.bfloat16)


def global_rows(query_rows, key_tokens, value_tokens):
    scores = jnp.einsum("qhs,khs->hqk", query_rows.astype(jnp.float32), key_tokens.astype(jnp.float32)) * (HEAD_DIM ** -0.5)
    weights = soft_weights(scores)
    return jnp.einsum("hqk,khs->qhs", weights.astype(jnp.float32), value_tokens.astype(jnp.float32)).astype(jnp.bfloat16)


def reference(queries, key_states, value_states, random_blocks, global_blocks):
    results = []
    per_step = math.gcd(NBLK, 8)
    step_count = NBLK // per_step
    for document in range(DOCS):
        query_blocks = queries[document].reshape(NBLK, BLOCK, HEADS, HEAD_DIM)
        key_blocks = key_states[document].reshape(NBLK, BLOCK, HEADS, HEAD_DIM)
        value_blocks = value_states[document].reshape(NBLK, BLOCK, HEADS, HEAD_DIM)
        indices = jnp.arange(NBLK, dtype=jnp.int32)
        globals_here = global_blocks[document].astype(jnp.int32)
        listed = jnp.concatenate([jnp.broadcast_to(globals_here[None, :], (NBLK, NGLOB)), (indices - 1)[:, None], indices[:, None], (indices + 1)[:, None], random_blocks[document].astype(jnp.int32)], axis=1)
        live_mask = jnp.concatenate([jnp.ones((NBLK, NGLOB), jnp.bool_), (indices >= 1)[:, None], jnp.ones((NBLK, 1), jnp.bool_), (indices + 1 < NBLK)[:, None], jnp.ones((NBLK, NRAND), jnp.bool_)], axis=1)
        listed = jnp.clip(listed, 0, NBLK - 1).astype(jnp.int32)

        def one_group(packed):
            query_group, listed_group, live_group = packed
            gathered_keys = jnp.take(key_blocks, listed_group, axis=0).reshape(per_step, -1, HEADS, HEAD_DIM)
            gathered_values = jnp.take(value_blocks, listed_group, axis=0).reshape(per_step, -1, HEADS, HEAD_DIM)
            scores = jnp.einsum("pqhs,pkhs->phqk", query_group.astype(jnp.float32), gathered_keys.astype(jnp.float32)) * (HEAD_DIM ** -0.5)
            live_tokens = jnp.repeat(live_group, BLOCK, axis=1)
            scores = jnp.where(live_tokens[:, None, None, :], scores, -1e30)
            weights = soft_weights(scores)
            return jnp.einsum("phqk,pkhs->pqhs", weights.astype(jnp.float32), gathered_values.astype(jnp.float32)).astype(jnp.bfloat16)

        local = lax.map(one_group, (query_blocks.reshape(step_count, per_step, BLOCK, HEADS, HEAD_DIM), listed.reshape(step_count, per_step, -1), live_mask.reshape(step_count, per_step, -1)))
        local = local.reshape(NBLK, BLOCK, HEADS, HEAD_DIM)
        key_tokens = key_states[document].reshape(LEN, HEADS, HEAD_DIM)
        value_tokens = value_states[document].reshape(LEN, HEADS, HEAD_DIM)
        for slot_index in range(NGLOB):
            where_block = globals_here[slot_index]
            rows_here = lax.dynamic_index_in_dim(query_blocks, where_block, 0, keepdims=False)
            local = lax.dynamic_update_index_in_dim(local, global_rows(rows_here, key_tokens, value_tokens), where_block, 0)
        results.append(local.reshape(LEN, ATT))
    return jnp.stack(results)
```

```python
import functools
import math

import jax
import jax.numpy as jnp
from jax import lax
from jax.experimental import pallas as pl
from jax.experimental.pallas import tpu as pltpu
from jax.sharding import PartitionSpec as P

HEAD_DIM = 128
BLOCK = 64
NGLOB = 2
NRAND = 3


def from_partner(block, axis, distance):
    count = lax.axis_size(axis)
    route = []
    for low in range(count):
        high = low | 1 << distance
        if high != low and high < count:
            route += [(low, high), (high, low)]
    return lax.ppermute(block, axis, route)


def soft_weights(scores):
    row_max = jnp.max(scores, axis=-1, keepdims=True)
    exponent = jnp.exp(scores - row_max)
    return (exponent / jnp.sum(exponent, axis=-1, keepdims=True)).astype(jnp.bfloat16)


def global_rows(query_rows, key_tokens, value_tokens):
    scores = jnp.einsum(
        "qhs,khs->hqk", query_rows, key_tokens, preferred_element_type=jnp.float32
    ) * HEAD_DIM ** (-0.5)
    weights = soft_weights(scores)
    return jnp.einsum(
        "hqk,khs->qhs", weights, value_tokens, preferred_element_type=jnp.float32
    ).astype(jnp.bfloat16)


def per_device(queries, key_states, value_states, random_blocks, global_blocks):
    devices = lax.axis_size("seq")
    device = lax.axis_index("seq")
    documents = queries.shape[0]
    head_groups = devices // (2 * documents)
    group_width = queries.shape[2] // head_groups
    heads_here = group_width // HEAD_DIM
    block_len = BLOCK
    total_blocks = 2 * devices
    parity = device % 2
    document = device // (2 * head_groups)

    def by_parity(states):
        pieces = states.reshape(documents, 2, block_len, head_groups, group_width)
        return pieces.transpose(0, 3, 1, 2, 4).reshape(devices, block_len, group_width)

    query_recv, key_half, value_half = (
        lax.all_to_all(by_parity(queries), "seq", split_axis=0, concat_axis=1, tiled=True),
        lax.all_to_all(by_parity(key_states), "seq", split_axis=0, concat_axis=1, tiled=True),
        lax.all_to_all(by_parity(value_states), "seq", split_axis=0, concat_axis=1, tiled=True),
    )
    key_other, value_other = from_partner((key_half, value_half), "seq", 0)

    def alternate(own_rows, their_rows):
        own_rows = own_rows.reshape(devices, 1, block_len, group_width)
        their_rows = their_rows.reshape(devices, 1, block_len, group_width)
        joined = jnp.where(
            parity == 0,
            jnp.concatenate([own_rows, their_rows], axis=1),
            jnp.concatenate([their_rows, own_rows], axis=1),
        )
        return joined.reshape(total_blocks * block_len, group_width)

    key_flat = alternate(key_half, key_other)
    value_flat = alternate(value_half, value_other)
    key_blocks = key_flat.reshape(total_blocks, block_len, heads_here, HEAD_DIM)
    value_blocks = value_flat.reshape(total_blocks, block_len, heads_here, HEAD_DIM)
    key_tokens = key_flat.reshape(total_blocks * block_len, heads_here, HEAD_DIM)
    value_tokens = value_flat.reshape(total_blocks * block_len, heads_here, HEAD_DIM)
    query_mine = query_recv.reshape(devices, block_len, heads_here, HEAD_DIM)
    document_lists = lax.dynamic_index_in_dim(random_blocks, document, 0, keepdims=False)
    own_lists = lax.dynamic_index_in_dim(
        document_lists.reshape(devices, 2, NRAND), parity, 1, keepdims=False
    )
    globals_here = lax.dynamic_index_in_dim(global_blocks, document, 0, keepdims=False)
    positions = 2 * jnp.arange(devices, dtype=jnp.int32) + parity
    listed = jnp.concatenate(
        [
            jnp.broadcast_to(globals_here[None, :], (devices, NGLOB)),
            (positions - 1)[:, None],
            positions[:, None],
            (positions + 1)[:, None],
            own_lists,
        ],
        axis=1,
    )
    live_mask = jnp.concatenate(
        [
            jnp.ones((devices, NGLOB), jnp.bool_),
            (positions >= 1)[:, None],
            jnp.ones((devices, 1), jnp.bool_),
            (positions + 1 < total_blocks)[:, None],
            jnp.ones((devices, NRAND), jnp.bool_),
        ],
        axis=1,
    )
    listed = jnp.clip(listed, 0, total_blocks - 1)
    per_step = math.gcd(devices, max(1, 512 // block_len))
    step_count = devices // per_step

    def local_group(packed):
        query_group, listed_group, live_group = packed
        gathered_keys = jnp.take(key_blocks, listed_group, axis=0).reshape(
            per_step, -1, heads_here, HEAD_DIM
        )
        gathered_values = jnp.take(value_blocks, listed_group, axis=0).reshape(
            per_step, -1, heads_here, HEAD_DIM
        )
        scores = jnp.einsum(
            "pqhs,pkhs->phqk", query_group, gathered_keys, preferred_element_type=jnp.float32
        ) * HEAD_DIM ** (-0.5)
        live_tokens = jnp.repeat(live_group, block_len, axis=1)
        scores = jnp.where(live_tokens[:, None, None, :], scores, -1e30)
        weights = soft_weights(scores)
        return jnp.einsum(
            "phqk,pkhs->pqhs", weights, gathered_values, preferred_element_type=jnp.float32
        ).astype(jnp.bfloat16)

    attended = lax.map(
        local_group,
        (
            query_mine.reshape(step_count, per_step, block_len, heads_here, HEAD_DIM),
            listed.reshape(step_count, per_step, -1),
            live_mask.reshape(step_count, per_step, -1),
        ),
    )
    attended = attended.reshape(devices, block_len, heads_here, HEAD_DIM)
    owned = [globals_here[slot_index] % 2 == parity for slot_index in range(NGLOB)]
    places = [globals_here[slot_index] // 2 for slot_index in range(NGLOB)]
    for slot_index in range(NGLOB):
        place_here = places[slot_index]

        def compute_rows(current):
            rows_here = lax.dynamic_index_in_dim(query_mine, place_here, 0, keepdims=False)
            return lax.dynamic_update_index_in_dim(
                current, global_rows(rows_here, key_tokens, value_tokens), place_here, 0
            )

        def keep_rows(current):
            return current

        attended = lax.cond(owned[slot_index], compute_rows, keep_rows, attended)
    returned = lax.all_to_all(
        attended.reshape(devices, block_len, group_width),
        "seq",
        split_axis=0,
        concat_axis=0,
        tiled=True,
    )
    returned = returned.reshape(documents, head_groups, 2, block_len, group_width).transpose(
        0, 2, 3, 1, 4
    )
    return returned.reshape(documents, 2 * block_len, head_groups * group_width)


SCALE = HEAD_DIM ** (-0.5)
MESH = pl.DeviceIdType.MESH


def fused_kernel(
    devices, heads_here, random_ref, global_ref, q_in, k_in, v_in, out_ref,
    q_buf, k_buf, v_buf, o_buf, wide_rows, in_send, in_recv, out_send, out_recv, own_sem,
):
    documents, blocks_here, _, width = q_in.shape
    chunks = documents * heads_here
    total_blocks = devices * blocks_here
    half = devices // 2
    me = lax.axis_index("seq")
    side = me // half

    def partner(step):
        return (side + 1 + step // half) % 2 * half + (me + step) % half

    barrier = pltpu.get_barrier_semaphore()

    def greet(step, carry):
        @pl.when(step != half)
        def _():
            pl.semaphore_signal(barrier, inc=1, device_id={"seq": partner(step)}, device_id_type=MESH)

        return carry

    arrays = ((q_in, q_buf), (k_in, k_buf), (v_in, v_buf))

    def own_in(chunk, index):
        source, target = arrays[index]
        column = pl.multiple_of((me * heads_here + chunk % heads_here) * HEAD_DIM, HEAD_DIM)
        return pltpu.make_async_copy(
            source.at[chunk // heads_here, :, :, pl.ds(column, HEAD_DIM)],
            target.at[chunk, pl.ds(me * blocks_here, blocks_here)],
            own_sem.at[index, chunk],
        )

    def own_out(chunk):
        column = pl.multiple_of((me * heads_here + chunk % heads_here) * HEAD_DIM, HEAD_DIM)
        return pltpu.make_async_copy(
            o_buf.at[chunk, pl.ds(me * blocks_here, blocks_here)],
            out_ref.at[chunk // heads_here, :, :, pl.ds(column, HEAD_DIM)],
            own_sem.at[3, chunk],
        )

    def send_in(place, carry):
        chunk, step = place // devices, place % devices

        @pl.when(step != half)
        def _():
            target_device = partner(step)
            column = pl.multiple_of(
                (target_device * heads_here + chunk % heads_here) * HEAD_DIM, HEAD_DIM
            )
            for index, (source, target) in enumerate(arrays):
                pltpu.make_async_remote_copy(
                    src_ref=source.at[chunk // heads_here, :, :, pl.ds(column, HEAD_DIM)],
                    dst_ref=target.at[chunk, pl.ds(me * blocks_here, blocks_here)],
                    send_sem=in_send.at[index],
                    recv_sem=in_recv.at[index, chunk],
                    device_id={"seq": target_device},
                    device_id_type=MESH,
                ).start()

        return carry

    for chunk in range(chunks):
        for index in range(3):
            own_in(chunk, index).start()
    lax.fori_loop(0, devices, greet, 0)
    pl.semaphore_wait(barrier, devices - 1)
    lax.fori_loop(0, chunks * devices, send_in, 0)

    other_blocks = (devices - 1) * blocks_here
    lanes = lax.broadcasted_iota(jnp.int32, (1, (NGLOB + 3 + NRAND) * BLOCK), 1) // BLOCK

    def arrived(ref, send_sem, recv_sem):
        return pltpu.make_async_remote_copy(
            src_ref=ref, dst_ref=ref, send_sem=send_sem, recv_sem=recv_sem,
            device_id={"seq": partner(0)}, device_id_type=MESH,
        )

    def softmax_values(scores, values):
        row_max = jnp.max(scores, axis=-1, keepdims=True)
        exponent = jnp.exp((scores - row_max) * SCALE)
        total = jnp.sum(exponent, axis=-1, keepdims=True)
        mixed = jnp.dot(exponent.astype(jnp.bfloat16), values, preferred_element_type=jnp.float32)
        return (mixed / total).astype(jnp.bfloat16)

    def products(left, right):
        return lax.dot_general(
            left, right, (((1,), (1,)), ((), ())), preferred_element_type=jnp.float32
        )

    def block_at(ref, chunk, block):
        return ref[chunk, block]

    def attend(chunk, carry):
        document = chunk // heads_here
        globals_here = [global_ref[document, slot] for slot in range(NGLOB)]
        for slot in range(NGLOB):
            wide_rows[slot] = softmax_values(
                products(block_at(q_buf, chunk, globals_here[slot]), k_buf[chunk].reshape(-1, HEAD_DIM)),
                v_buf[chunk].reshape(-1, HEAD_DIM),
            )

        def owner(step, inner):
            target_device = partner(step)
            for offset in range(blocks_here):
                block = target_device * blocks_here + offset
                listed = globals_here + [
                    jnp.maximum(block - 1, 0), block, jnp.minimum(block + 1, total_blocks - 1)
                ] + [
                    random_ref[document, block * NRAND + pick] for pick in range(NRAND)
                ]
                keys = jnp.concatenate([block_at(k_buf, chunk, item) for item in listed], axis=0)
                values = jnp.concatenate([block_at(v_buf, chunk, item) for item in listed], axis=0)
                scores = products(block_at(q_buf, chunk, block), keys)
                dead = ((lanes == NGLOB) & (block == 0)) | (
                    (lanes == NGLOB + 2) & (block == total_blocks - 1)
                )
                mixed = softmax_values(jnp.where(dead, -1e30, scores), values)
                for slot in range(NGLOB):
                    mixed = jnp.where(
                        jnp.full(mixed.shape, globals_here[slot]) == block, wide_rows[slot], mixed
                    )
                o_buf[chunk, block] = mixed

            @pl.when(step != half)
            def _():
                column = pl.multiple_of(
                    (me * heads_here + chunk % heads_here) * HEAD_DIM, HEAD_DIM
                )
                pltpu.make_async_remote_copy(
                    src_ref=o_buf.at[chunk, pl.ds(target_device * blocks_here, blocks_here)],
                    dst_ref=out_ref.at[document, :, :, pl.ds(column, HEAD_DIM)],
                    send_sem=out_send,
                    recv_sem=out_recv,
                    device_id={"seq": target_device},
                    device_id_type=MESH,
                ).start()

            @pl.when(step == half)
            def _():
                own_out(chunk).start()

            return inner

        lax.fori_loop(0, devices, owner, 0)
        return carry

    for chunk in range(chunks):
        for index, (source, target) in enumerate(arrays):
            own_in(chunk, index).wait()
            arrived(
                target.at[chunk, pl.ds(0, other_blocks)], in_send.at[index], in_recv.at[index, chunk]
            ).wait_recv()
    lax.fori_loop(0, chunks, attend, 0)
    other_width = (devices - 1) * (width // devices)
    for chunk in range(chunks):
        own_out(chunk).wait()
    for index, (source, target) in enumerate(arrays):
        arrived(
            source.at[:, :, :, pl.ds(0, other_width)], in_send.at[index], in_recv.at[index, 0]
        ).wait_send()
    arrived(o_buf.at[:, pl.ds(0, other_blocks)], out_send, out_recv).wait_send()
    arrived(out_ref.at[:, :, :, pl.ds(0, other_width)], out_send, out_recv).wait_recv()


def fused(queries, key_states, value_states, random_blocks, global_blocks):
    devices = lax.axis_size("seq")
    documents, rows, width = queries.shape
    heads_here = width // HEAD_DIM // devices
    chunks = documents * heads_here
    blocked = (documents, rows // BLOCK, BLOCK, width)
    gathered = pltpu.VMEM((chunks, devices * rows // BLOCK, BLOCK, HEAD_DIM), jnp.bfloat16)
    anywhere = pl.BlockSpec(memory_space=pl.ANY)
    scalars = pl.BlockSpec(memory_space=pltpu.SMEM)
    return pl.pallas_call(
        functools.partial(fused_kernel, devices, heads_here),
        out_shape=jax.ShapeDtypeStruct(blocked, queries.dtype),
        in_specs=[scalars, scalars, anywhere, anywhere, anywhere],
        out_specs=anywhere,
        scratch_shapes=[
            gathered, gathered, gathered, gathered,
            pltpu.VMEM((NGLOB, BLOCK, HEAD_DIM), jnp.bfloat16),
            pltpu.SemaphoreType.DMA((3,)),
            pltpu.SemaphoreType.DMA((3, chunks)),
            pltpu.SemaphoreType.DMA,
            pltpu.SemaphoreType.DMA,
            pltpu.SemaphoreType.DMA((4, chunks)),
        ],
        compiler_params=pltpu.CompilerParams(collective_id=0, has_side_effects=True),
    )(
        random_blocks.reshape(documents, -1), global_blocks,
        queries.reshape(blocked), key_states.reshape(blocked), value_states.reshape(blocked),
    ).reshape(queries.shape)


def per_device_any(queries, key_states, value_states, random_blocks, global_blocks):
    devices = lax.axis_size("seq")
    heads = queries.shape[2] // HEAD_DIM
    if devices % 2 == 0 and heads % devices == 0 and queries.shape[1] % BLOCK == 0:
        return fused(queries, key_states, value_states, random_blocks, global_blocks)
    return per_device(queries, key_states, value_states, random_blocks, global_blocks)


def solution(mesh):
    placed = (
        P("groups", "seq", None),
        P("groups", "seq", None),
        P("groups", "seq", None),
        P("groups", None, None),
        P("groups", None),
    )
    return jax.shard_map(
        per_device_any, mesh=mesh, in_specs=placed, out_specs=P("groups", "seq", None), check_vma=False
    )
```
